512 devices in a mesh: rows: 64 (over z, y), feat: 8 (over x, core).
Axes of the slice: x: 4, y: 8, z: 8, core: 2. Of those that a mesh axis runs over, the one named last changes fastest.
Arguments:
- bin_ids: int32 [512, 131072], P('feat', 'rows'), may hold values from 0 to 255
- leaf_ids: int32 [131072], P('rows'), may hold values from 0 to 63
- gradient: float32 [131072], P('rows'), may hold values from -6 to 6
- hessian: float32 [131072], P('rows'), may hold values from 0.01 to 0.25
- raw_feats: bfloat16 [131072, 64], P(('rows', 'feat')), may hold values from -6 to 6
- prior_score: float32 [131072], P(('rows', 'feat')), may hold values from -6 to 6
- elected: int32 [64, 64], P(None, 'feat'), may hold values from 0 to 63, as said below
Outputs:
- relative_gain: float32 [64, 64, 256], P('rows', 'feat')
- coefficients: float32 [64, 65], P('rows')
- new_score: float32 [131072], P(('rows', 'feat'))
The draws below stay inside these ranges and needn't reach their ends.
Inputs may be any that keep to these rules, and one draw needn't show every extreme that they name: `elected`: within each row, each group's 8 entries are distinct feature numbers of that group.
All inputs are finite; a program needn't handle non-finite values.
Results may differ from the reference program's by a relative error of at most 0.0029.
Values sent between devices are 32-bit elements; how exact they have to be, the bound alone decides.
A program may use at most 64 MiB of HBM per device.

```python
import math
import jax
import jax.numpy as jnp
import numpy as np
from jax import lax

BINS = 256
F_DEV = 64
RAW = 64
LEAVES = 64
KV = 8
ROW_DEV = 2048
F = 512
ELECTED = 64
ROWS = 131072
N_FEAT = 8


def draw_elected(key, part):
    scores = jax.random.randint(key, (LEAVES, N_FEAT, F_DEV), 0, 1 << 20)
    scores = scores * F_DEV + lax.broadcasted_iota(jnp.int32, (LEAVES, N_FEAT, F_DEV), 2)
    scores = scores.at[0, :, F_DEV - 1].set(-2)
    scores = scores.at[1, :, 0].set(-1)
    picked = jnp.argsort(scores, axis=2)[:, :, :KV]
    return picked.reshape(LEAVES, N_FEAT * KV).astype(jnp.int32)


def place_ends(entries, key, least, high):
    dims = entries.shape
    spot = [jax.random.randint(jax.random.fold_in(key, axis), (), 0, dims[axis]) for axis in range(len(dims))]
    entries = entries.at[tuple(spot)].set(least)
    longest = dims.index(max(dims))
    spot[longest] = (spot[longest] + 1) % dims[longest]
    return entries.at[tuple(spot)].set(high)


def steps_of(rng, extent, cuts, low, high):
    def one(axis_at, parts):
        heights = jax.random.uniform(jax.random.fold_in(jax.random.fold_in(rng, 6), axis_at), (parts,), jnp.float32, low / len(cuts), high / len(cuts))
        return jnp.repeat(jnp.exp(heights), extent[axis_at] // parts).reshape((-1,) + (1,) * (len(extent) - axis_at - 1))

    factor_of = one(*cuts[0])
    for cut in cuts[1:]:
        factor_of = factor_of * one(*cut)
    return factor_of


def cumulative_ranks(number_of, slope):
    loads = [(1 << 20) // math.isqrt(rank ** slope) + 1 for rank in range(1, number_of + 1)]
    deviation = 1 + sum(loads) // (1 << 30)
    return np.cumsum(np.array([max(1, weight // deviation) for weight in loads]))


def ranked(rng, shape, number_of, slope):
    listing = cumulative_ranks(number_of, slope)
    pick = jax.random.randint(jax.random.fold_in(rng, 1), shape, 0, int(listing[number_of - 1]))
    standing = jnp.searchsorted(jnp.asarray(listing, jnp.int32), pick, side="right")
    return jax.random.permutation(jax.random.fold_in(rng, 2), number_of)[standing].astype(jnp.int32)


def scatter_about(key, extent, scale, bound, cuts=(), kind=jnp.bfloat16):
    factor_of = steps_of(key, extent, cuts, -0.22, 0.18) if cuts else 1.0
    drawn = jax.random.normal(key, extent, jnp.float32) * scale * factor_of
    return jnp.minimum(jnp.maximum(drawn, -bound), bound).astype(kind)


def setup_inputs(seed: int = 0) -> dict:
    streams_of = jax.random.split(jax.random.key(seed), 8)
    bin_ids = place_ends(jax.random.randint(streams_of[0], (F, ROWS), 0, BINS), jax.random.fold_in(streams_of[0], 1), 0, BINS - 1).astype(jnp.int32)
    leaf_ids = place_ends(ranked(streams_of[1], (ROWS,), LEAVES, 1), jax.random.fold_in(streams_of[1], 3), 0, LEAVES - 1).astype(jnp.int32)
    gradient = scatter_about(streams_of[2], (ROWS,), 1.0, 6.0, ((0, 64),), jnp.float32)
    hessian = jnp.clip(jnp.exp(math.log(0.25) - 3.218876 * jax.random.uniform(streams_of[3], (ROWS,), jnp.float32) ** steps_of(streams_of[3], (ROWS,), ((0, 64),), -0.2, 0.2)), 0.01, 0.25)
    raw_feats = scatter_about(streams_of[4], (ROWS, RAW), 1.0, 6.0, ((0, 512),))
    prior_score = scatter_about(streams_of[5], (ROWS,), 1.0, 6.0, ((0, 512),), jnp.float32)
    elected = draw_elected(jax.random.fold_in(streams_of[7], 71), 0)
    return {"bin_ids": bin_ids, "leaf_ids": leaf_ids, "gradient": gradient, "hessian": hessian, "raw_feats": raw_feats, "prior_score": prior_score, "elected": elected}


SPLIT_REG = 1.0
RIDGE_REG = 1.0
SHRINKAGE = 0.3

def split_gains(hist_grad, hist_hess):
    left_grad = jnp.cumsum(hist_grad, axis=-1)
    left_hess = jnp.cumsum(hist_hess, axis=-1)
    total_grad = left_grad[..., -1:]
    total_hess = left_hess[..., -1:]
    right_grad = total_grad - left_grad
    first = left_grad * left_grad / (left_hess + SPLIT_REG)
    second = right_grad * right_grad / (total_hess - left_hess + SPLIT_REG)
    whole = total_grad * total_grad / (total_hess + SPLIT_REG)
    return first + second - whole

def solve_leaves(blocks):
    width = blocks.shape[2]
    system = blocks[:, :width, :] + RIDGE_REG * jnp.eye(width, dtype=blocks.dtype)
    target = blocks[:, width:, :]
    factor = jnp.linalg.cholesky(system)
    middle = lax.linalg.triangular_solve(factor, target, left_side=False, lower=True, transpose_a=True)
    answer = lax.linalg.triangular_solve(factor, middle, left_side=False, lower=True, transpose_a=False)
    return -answer[:, 0, :]

def reference(bin_ids, leaf_ids, gradient, hessian, raw_feats, prior_score, elected):
    grad_round = lax.optimization_barrier(gradient.astype(jnp.bfloat16)).astype(jnp.float32)
    hess_round = lax.optimization_barrier(hessian.astype(jnp.bfloat16)).astype(jnp.float32)
    slots = jnp.arange(ELECTED, dtype=jnp.int32)
    feature = (slots // KV * F_DEV)[None, :] + elected
    row_feature = feature[leaf_ids].astype(jnp.int32)
    row_index = jnp.arange(ROWS, dtype=jnp.int32)[:, None]
    chosen = bin_ids[row_feature, row_index]
    codes = ((leaf_ids[:, None] * ELECTED + slots[None, :]) * BINS + chosen).reshape(-1).astype(jnp.int32)
    segments = LEAVES * ELECTED * BINS
    grad_flat = jnp.broadcast_to(grad_round[:, None], (ROWS, ELECTED)).reshape(-1)
    hess_flat = jnp.broadcast_to(hess_round[:, None], (ROWS, ELECTED)).reshape(-1)
    hist_grad = jax.ops.segment_sum(grad_flat, codes, num_segments=segments).reshape(LEAVES, ELECTED, BINS)
    hist_hess = jax.ops.segment_sum(hess_flat, codes, num_segments=segments).reshape(LEAVES, ELECTED, BINS)
    gains = split_gains(hist_grad, hist_hess)
    best = jnp.max(gains, axis=(1, 2))
    relative_gain = gains - best[:, None, None]
    unit_column = jnp.ones((ROWS, 1), jnp.float32)
    augmented = jnp.concatenate([raw_feats.astype(jnp.float32), unit_column], axis=1)
    weighted = lax.optimization_barrier((hessian[:, None] * augmented).astype(jnp.bfloat16)).astype(jnp.float32)
    extended = jnp.concatenate([weighted, grad_round[:, None]], axis=1)
    block_count = ROWS // ROW_DEV

    def accumulate(carry, pieces):
        ext_piece, aug_piece, leaf_piece = pieces
        outer = ext_piece[:, :, None] * aug_piece[:, None, :]
        return (carry + jax.ops.segment_sum(outer, leaf_piece, num_segments=LEAVES), None)
    start_blocks = jnp.zeros((LEAVES, RAW + 2, RAW + 1), jnp.float32)
    blocks = lax.scan(accumulate, start_blocks, (extended.reshape(block_count, ROW_DEV, RAW + 2), augmented.reshape(block_count, ROW_DEV, RAW + 1), leaf_ids.reshape(block_count, ROW_DEV)))[0]
    coefficients = solve_leaves(blocks)
    new_score = prior_score + SHRINKAGE * jnp.sum(augmented * coefficients[leaf_ids], axis=1)
    return (relative_gain, coefficients, new_score)
```

```python
import functools

import jax
import jax.numpy as jnp
from jax import lax
from jax.experimental import pallas as pl
from jax.experimental.pallas import tpu as pltpu
from jax.sharding import PartitionSpec as P

BINS = 256
CORES = 2
HALF = 4
PACK = 40
LANES = 128
SPLIT_REG = 1.0
RIDGE_REG = 1.0
SHRINKAGE = 0.3
MESH = pl.DeviceIdType.MESH
NT = (((1,), (1,)), ((), ()))
NN = (((1,), (0,)), ((), ()))
F32 = jnp.float32
BF16 = jnp.bfloat16


def dot(a, b, dims):
    return lax.dot_general(a, b, dims, preferred_element_type=F32)


def iota(shape, axis):
    return lax.broadcasted_iota(jnp.int32, shape, axis)


def split3(v):
    hi = v.astype(BF16)
    rest = v - hi.astype(F32)
    mid = rest.astype(BF16)
    return hi, mid, (rest - mid.astype(F32)).astype(BF16)


def kernel(
    dims, bins_ref, leaf_ref, grad_ref, hess_ref, raw_ref, prior_ref, elect_ref,
    gain_ref, coef_ref, score_ref,
    xt, chosen, wmat, hist, ring, spread, gathered, xb, wb, lhs,
    parts, gram_z, gram_send, gram_y, square, coef_z, coef_f, tops,
    sx, rx, sring, rring, sh, rh, sgz, rgz, sgy, rgy, scz, rcz, scf, rcf, stp, rtp,
):
    nz, ny, nf = dims
    nx = nf // CORES
    leaves = nz * ny
    rows = leaf_ref.shape[1]
    group = rows // nf
    row_pos = lax.axis_index("rows")
    f = lax.axis_index("feat")
    z, y = row_pos // ny, row_pos % ny
    x, core = f // CORES, f % CORES

    def at_z(k):
        return (lax.rem(z + k + nz, nz) * ny + y, f)

    def at_y(k):
        return (z * ny + lax.rem(y + k + ny, ny), f)

    def at_f(k):
        return (row_pos, lax.rem(f + k + nf, nf))

    started = []

    def send(src, dst, ssem, rsem, dev):
        copy = pltpu.make_async_remote_copy(
            src_ref=src, dst_ref=dst, send_sem=ssem, recv_sem=rsem,
            device_id=dev, device_id_type=MESH,
        )
        copy.start()
        started.append(copy)

    def arrive(dst, ssem, rsem):
        pltpu.make_async_remote_copy(
            src_ref=dst, dst_ref=dst, send_sem=ssem, recv_sem=rsem,
            device_id=(row_pos, f), device_id_type=MESH,
        ).wait_recv()

    barrier = pltpu.get_barrier_semaphore()
    for k in range(1, nf):
        pl.semaphore_signal(barrier, inc=1, device_id=at_f(k), device_id_type=MESH)
    for k in range(1, nz):
        pl.semaphore_signal(barrier, inc=1, device_id=at_z(k), device_id_type=MESH)
    for k in range(1, ny):
        pl.semaphore_signal(barrier, inc=1, device_id=at_y(k), device_id_type=MESH)

    feats = raw_ref.shape[1]
    eye = (iota((feats, feats), 0) == iota((feats, feats), 1)).astype(F32).astype(BF16)
    xt[f] = dot(eye, raw_ref[...], NT)

    leaf = leaf_ref[...]
    grad = grad_ref[...].astype(BF16).astype(F32)
    hess = hess_ref[...].astype(BF16).astype(F32)

    slots = elect_ref.shape[1]
    eye = (iota((slots, slots), 0) == iota((slots, slots), 1)).astype(F32).astype(BF16)
    table = dot(eye, elect_ref[...].astype(F32).astype(BF16), NT).astype(BF16)
    member = (iota((leaves, rows), 0) == leaf).astype(F32).astype(BF16)
    picked = dot(table, member, NN).astype(jnp.int32)
    bins = bins_ref[...]
    number = iota(bins.shape, 0)
    for e in range(slots):
        row = jnp.where(number == picked[e : e + 1, :], bins, 0)
        chosen[e : e + 1, :] = jnp.sum(row, axis=0, keepdims=True).astype(F32)

    pl.semaphore_wait(barrier, (nf - 1) + (nz - 1) + (ny - 1))

    mate = (row_pos, x * CORES + (1 - core))
    for d in range(1, nx):
        dev = (row_pos, lax.rem(x + d, nx) * CORES + core)
        send(xt.at[f], xt.at[f], sx.at[d - 1], rx.at[d - 1], dev)
    send(xt.at[f], xt.at[f], sx.at[nx - 1], rx.at[nx - 1], mate)

    def weigh(d, carry):
        first = leaf == d * ny + iota((ny, rows), 0)
        both = [jnp.where(first, grad, 0.0), jnp.where(first, hess, 0.0)]
        at = pl.multiple_of(d * (2 * ny), 2 * ny)
        wmat[0, pl.ds(at, 2 * ny), :] = jnp.concatenate(both, axis=0).astype(BF16)
        return carry

    lax.fori_loop(0, nz, weigh, 0)

    def weigh_y(d, carry):
        first = leaf == iota((nz, rows), 0) * ny + d
        both = [jnp.where(first, grad, 0.0), jnp.where(first, hess, 0.0)]
        at = pl.multiple_of(d * (2 * nz), 2 * nz)
        wmat[1, pl.ds(at, 2 * nz), :] = jnp.concatenate(both, axis=0).astype(BF16)
        return carry

    lax.fori_loop(0, ny, weigh_y, 0)

    def count(e, carry):
        row = chosen[pl.ds(e, 1), :]
        onehot = (iota((BINS, rows), 0).astype(F32) == row).astype(F32).astype(BF16)
        hist[e] = dot(wmat[e // HALF], onehot, NT)
        return carry

    lax.fori_loop(0, slots, count, 0)

    axes = ((nz, z, at_z, 2 * ny), (ny, y, at_y, 2 * nz))

    def piece(h, part, dest, tall):
        at = pl.multiple_of(dest * tall, tall)
        return hist.at[pl.ds(h * HALF + part * 2, 2), pl.ds(at, tall), :]

    def ring_step(s):
        for h, (n, me, peer, tall) in enumerate(axes):
            far = n // 2
            if s > far:
                continue
            dist = far + 1 - s
            for way, sign in enumerate((1, -1)):
                dest = lax.rem(me + sign * dist + n, n)
                for part in range(2):
                    most = far if part == way else far - 1
                    if dist > most:
                        continue
                    src = piece(h, part, dest, tall)
                    if dist < most:
                        held = ring.at[h, way, part, s - 2]
                        arrive(held, sring.at[h, way, part, s - 2], rring.at[h, way, part, s - 2])
                        held[...] += src[...]
                        src = held
                    send(
                        src, ring.at[h, way, part, s - 1], sring.at[h, way, part, s - 1],
                        rring.at[h, way, part, s - 1], peer(sign),
                    )

    ring_step(1)

    for d in range(1, nx):
        at = lax.rem(x - d + nx, nx) * CORES + core
        arrive(xt.at[at], sx.at[d - 1], rx.at[d - 1])
        send(xt.at[at], xt.at[at], sx.at[nx - 1 + d], rx.at[nx - 1 + d], mate)
    arrive(xt.at[f], sx.at[nx - 1], rx.at[nx - 1])
    for d in range(1, nx):
        at = lax.rem(x - d + nx, nx) * CORES + (1 - core)
        arrive(xt.at[at], sx.at[nx - 1 + d], rx.at[nx - 1 + d])
    for b in range(nf):
        block = xt[b]
        cut = pl.ds(b * group, group)
        scaled = hess_ref[:, cut] * block
        xb[:, cut] = block.astype(BF16)
        wb[0:feats, cut] = scaled.astype(BF16)
        for lz in range(nz):
            mine = leaf_ref[:, cut] == lz * ny + f
            lhs[lz * feats : (lz + 1) * feats, cut] = jnp.where(mine, scaled, 0.0).astype(BF16)
    tail = iota((16, rows), 0)
    wb[feats : feats + 16, :] = jnp.where(
        tail == 0, hess, jnp.where(tail == 1, grad, 0.0)
    ).astype(BF16)
    mine = leaf == iota((nz, rows), 0) * ny + f
    sides = [jnp.where(mine, hess, 0.0), jnp.where(mine, grad, 0.0)]
    if 2 * nz < 16:
        sides.append(jnp.zeros((16 - 2 * nz, rows), F32))
    side = dot(jnp.concatenate(sides, axis=0).astype(BF16), xb[...], NT)
    ones = jnp.concatenate([jnp.where(mine, 1.0, 0.0), jnp.zeros((16 - nz, rows), F32)], axis=0)
    last = dot(ones.astype(BF16), wb[...], NT)
    main = dot(lhs[...], xb[...], NT)
    fold = feats // 2
    for lz in range(nz):
        block = main[lz * feats : (lz + 1) * feats, :]
        parts[lz, 0:fold, :] = jnp.concatenate([block[:fold], block[fold:]], axis=1)
        parts[lz, fold : fold + 8, :] = jnp.zeros((8, LANES), F32)
        parts[lz, fold : fold + 1, 0:feats] = side[lz : lz + 1, :]
        parts[lz, fold + 1 : fold + 2, 0:feats] = side[nz + lz : nz + lz + 1, :]
        parts[lz, fold + 2 : fold + 3, 0 : feats + 16] = last[lz : lz + 1, :]
    for k in range(1, nz):
        to = lax.rem(z + k, nz)
        send(parts.at[to], gram_z.at[k - 1], sgz.at[k - 1], rgz.at[k - 1], at_z(k))

    for s in range(2, max(nz, ny) // 2 + 1):
        ring_step(s)

    total = parts[z]
    for k in range(1, nz):
        arrive(gram_z.at[k - 1], sgz.at[k - 1], rgz.at[k - 1])
        total = total + gram_z[k - 1]
    gram_send[...] = total
    for k in range(1, ny):
        send(gram_send, gram_y.at[k - 1], sgy.at[k - 1], rgy.at[k - 1], at_y(k))

    for h, (n, me, peer, tall) in enumerate(axes):
        other, peer2 = (ny, at_y) if h == 0 else (nz, at_z)
        for part in range(2):
            out = piece(h, part, me, tall)[...]
            for way in range(2):
                far = n // 2 if part == way else n // 2 - 1
                if far > 0:
                    at = (h, way, part, n // 2 - 1)
                    arrive(ring.at[at], sring.at[at], rring.at[at])
                    out = out + ring[at]
            for j in range(2):
                for gh in range(2):
                    slot = gh * HALF + part * 2 + j
                    for d in range(other):
                        spread[h, d, slot : slot + 1, :] = out[j, gh * other + d : gh * other + d + 1, :]
        here = y if h == 0 else z
        for k in range(1, other):
            to = lax.rem(here + k, other)
            send(spread.at[h, to], gathered.at[h, k - 1], sh.at[h, k - 1], rh.at[h, k - 1], peer2(k))

    for k in range(1, ny):
        arrive(gram_y.at[k - 1], sgy.at[k - 1], rgy.at[k - 1])
        total = total + gram_y[k - 1]
    left = iota((fold, LANES), 1) < feats
    square[...] = jnp.zeros((LANES, LANES), F32)
    square[0:fold, :] = jnp.where(left, total[0:fold], 0.0)
    square[fold:feats, :] = jnp.where(left, pltpu.roll(total[0:fold], LANES - feats, 1), 0.0)
    lane = iota((1, LANES), 1)
    ends = total[fold + 2 : fold + 3]
    square[feats : feats + 1, :] = jnp.where(lane < feats, total[fold : fold + 1] + ends, 0.0)
    square[feats + 1 : feats + 2, :] = jnp.where(lane < feats, total[fold + 1 : fold + 2], 0.0)
    square_t = square[...] + jnp.transpose(square[...])
    a = square_t[0:feats]
    lanes = iota((feats, LANES), 1)
    subs = iota((feats, LANES), 0)
    a = jnp.where(lanes <= feats, 0.5 * a, a) + jnp.where(lanes == subs, RIDGE_REG, 0.0)
    border = jnp.broadcast_to(a[:, feats : feats + 1], (feats, LANES))
    for k in range(0, feats, 2):
        c0 = jnp.broadcast_to(a[:, k : k + 1], (feats, LANES))
        c1 = jnp.broadcast_to(a[:, k + 1 : k + 2], (feats, LANES))
        r0, r1 = a[k : k + 1], a[k + 1 : k + 2]
        p00, p10 = c0[k : k + 1], c0[k + 1 : k + 2]
        p01, p11 = c1[k : k + 1], c1[k + 1 : k + 2]
        scale = 1.0 / (p00 * p11 - p01 * p10)
        n0 = (p11 * r0 - p01 * r1) * scale
        n1 = (p00 * r1 - p10 * r0) * scale
        a = a - c0 * n0 - c1 * n1
        a = jnp.where(subs == k, n0, jnp.where(subs == k + 1, n1, a))
    yc = jnp.broadcast_to(a[:, feats : feats + 1], (feats, LANES))
    yb = jnp.broadcast_to(a[:, feats + 1 : feats + 2], (feats, LANES))
    low = ends[:, feats : feats + 1] + RIDGE_REG - jnp.sum(border * yc, axis=0, keepdims=True)
    high = ends[:, feats + 1 : feats + 2] - jnp.sum(border * yb, axis=0, keepdims=True)
    const = high / low
    answer = jnp.sum(jnp.where(lanes == subs, yb - const * yc, 0.0), axis=0, keepdims=True)
    coef_z[z] = -jnp.where(lane == feats, const, answer)
    for k in range(1, nz):
        send(coef_z.at[z], coef_z.at[z], scz.at[k - 1], rcz.at[k - 1], at_z(k))

    upper = (iota((BINS, BINS), 0) <= iota((BINS, BINS), 1)).astype(F32).astype(BF16)
    gains = []
    for h in range(2):
        other = ny if h == 0 else nz
        sums = spread[h, y if h == 0 else z]
        for k in range(1, other):
            arrive(gathered.at[h, k - 1], sh.at[h, k - 1], rh.at[h, k - 1])
            sums = sums + gathered[h, k - 1]
        hi, mid, lo = split3(sums)
        run = dot(hi, upper, NN) + dot(mid, upper, NN) + dot(lo, upper, NN)
        lg, lh = run[0:HALF], run[HALF : 2 * HALF]
        tg, th = lg[:, BINS - 1 : BINS], lh[:, BINS - 1 : BINS]
        rg = tg - lg
        gains.append(
            lg * lg / (lh + SPLIT_REG) + rg * rg / (th - lh + SPLIT_REG) - tg * tg / (th + SPLIT_REG)
        )
    top = jnp.maximum(gains[0], gains[1])
    top = jnp.max(jnp.max(top, axis=1, keepdims=True), axis=0, keepdims=True)
    tops[f] = jnp.broadcast_to(top, (8, LANES))
    for k in range(1, nf):
        send(tops.at[f], tops.at[f], stp.at[k - 1], rtp.at[k - 1], at_f(k))

    for k in range(1, nz):
        at = lax.rem(z - k + nz, nz)
        arrive(coef_z.at[at], scz.at[k - 1], rcz.at[k - 1])
    for k in range(nz):
        coef_f[f, k : k + 1, :] = coef_z[k]
    for k in range(1, nf):
        send(coef_f.at[f], coef_f.at[f], scf.at[k - 1], rcf.at[k - 1], at_f(k))

    for k in range(1, nf):
        at = lax.rem(f - k + nf, nf)
        arrive(tops.at[at], stp.at[k - 1], rtp.at[k - 1])
    best = tops[0]
    for k in range(1, nf):
        best = jnp.maximum(best, tops[k])
    best = best[0:1, 0:1]
    for h in range(2):
        gain_ref[0, h * HALF : (h + 1) * HALF, :] = gains[h] - best

    for k in range(1, nf):
        at = lax.rem(f - k + nf, nf)
        arrive(coef_f.at[at], scf.at[k - 1], rcf.at[k - 1])
    coef_ref[...] = coef_f[y, pl.ds(z, 1), 0 : feats + 1]
    own = leaf_ref[:, pl.ds(pl.multiple_of(f * group, group), group)]
    tables = jnp.concatenate([coef_f[k] for k in range(nf)], axis=0)
    if leaves < LANES:
        tables = jnp.concatenate([tables, jnp.zeros((LANES - leaves, LANES), F32)], axis=0)
    column = jnp.transpose(tables)
    key = lax.rem(own, ny) * nz + own // ny
    pick = (iota((LANES, group), 0) == key).astype(F32).astype(BF16)
    hi, mid, lo = split3(column)
    per_row = dot(hi, pick, NN) + dot(mid, pick, NN) + dot(lo, pick, NN)
    value = jnp.sum(xt[f] * per_row[0:feats], axis=0, keepdims=True) + per_row[feats : feats + 1]
    score_ref[...] = prior_ref[...] + SHRINKAGE * value

    for copy in started:
        copy.wait_send()


def body(bin_ids, leaf_ids, gradient, hessian, raw_feats, prior_score, elected):
    rows = bin_ids.shape[1]
    leaves, slots = elected.shape
    nf = lax.axis_size("feat")
    ny = nf
    nz = lax.axis_size("rows") // ny
    group, feats = raw_feats.shape
    nx = nf // CORES
    far = max(nz, ny)
    tall = 2 * ny
    dma = pltpu.SemaphoreType.DMA
    vmem = pltpu.VMEM
    scratch = [
        vmem((nf, feats, group), F32),
        vmem((slots, rows), F32),
        vmem((2, 2 * leaves, rows), BF16),
        vmem((slots, 2 * leaves, BINS), F32),
        vmem((2, 2, 2, far // 2, 2, tall, BINS), F32),
        vmem((2, far, 2 * HALF, BINS), F32),
        vmem((2, far - 1, 2 * HALF, BINS), F32),
        vmem((feats, rows), BF16),
        vmem((feats + 16, rows), BF16),
        vmem((nz * feats, rows), BF16),
        vmem((nz, PACK, LANES), F32),
        vmem((nz - 1, PACK, LANES), F32),
        vmem((PACK, LANES), F32),
        vmem((ny - 1, PACK, LANES), F32),
        vmem((LANES, LANES), F32),
        vmem((nz, 1, LANES), F32),
        vmem((nf, nz, LANES), F32),
        vmem((nf, 8, LANES), F32),
    ]
    counts = [
        (2 * nx - 1,), (2, 2, 2, far // 2), (2, far - 1), (nz - 1,), (ny - 1,), (nz - 1,),
        (nf - 1,), (nf - 1,),
    ]
    for shape in counts:
        scratch += [dma(shape), dma(shape)]
    gain, coef, score = pl.pallas_call(
        functools.partial(kernel, (nz, ny, nf)),
        out_shape=(
            jax.ShapeDtypeStruct((1, slots, BINS), F32),
            jax.ShapeDtypeStruct((1, feats + 1), F32),
            jax.ShapeDtypeStruct((1, group), F32),
        ),
        in_specs=[pl.BlockSpec(memory_space=pltpu.VMEM)] * 7,
        out_specs=(pl.BlockSpec(memory_space=pltpu.VMEM),) * 3,
        scratch_shapes=scratch,
        compiler_params=pltpu.CompilerParams(
            collective_id=0, has_side_effects=True, vmem_limit_bytes=48 * 1024 * 1024
        ),
        name="level",
    )(
        bin_ids, leaf_ids.reshape(1, rows), gradient.reshape(1, rows), hessian.reshape(1, rows),
        raw_feats, prior_score.reshape(1, group), elected,
    )
    return gain, coef, score.reshape(group)


def solution(mesh):
    in_specs = (
        P("feat", "rows"),
        P("rows"),
        P("rows"),
        P("rows"),
        P(("rows", "feat"), None),
        P(("rows", "feat")),
        P(None, "feat"),
    )
    out_specs = (P("rows", "feat", None), P("rows", None), P(("rows", "feat")))
    return jax.shard_map(body, mesh=mesh, in_specs=in_specs, out_specs=out_specs, check_vma=False)
```

```python
import functools

import jax
import jax.numpy as jnp
from jax import lax
from jax.experimental import pallas as pl
from jax.experimental.pallas import tpu as pltpu
from jax.sharding import PartitionSpec as P

BINS = 256
CORES = 2
HALF = 4
PACK = 24
LANES = 128
SPLIT_REG = 1.0
RIDGE_REG = 1.0
SHRINKAGE = 0.3
MESH = pl.DeviceIdType.MESH
NT = (((1,), (1,)), ((), ()))
NN = (((1,), (0,)), ((), ()))
F32 = jnp.float32
BF16 = jnp.bfloat16


def dot(a, b, dims):
    return lax.dot_general(a, b, dims, preferred_element_type=F32)


def iota(shape, axis):
    return lax.broadcasted_iota(jnp.int32, shape, axis)


def split3(v):
    hi = v.astype(BF16)
    rest = v - hi.astype(F32)
    mid = rest.astype(BF16)
    return hi, mid, (rest - mid.astype(F32)).astype(BF16)


def kernel(
    dims, bins_hbm, leaf_hbm, grad_hbm, hess_hbm, raw_hbm, prior_hbm, elect_hbm,
    gain_ref, coef_ref, score_ref,
    bins_ref, leaf_ref, grad_ref, hess_ref, raw_ref, prior_ref, elect_ref, load_sem,
    xt, chosen, wmat, hist, ring, spread, gathered, xb, lhs,
    parts, gram_z, gram_send, gram_y, square, coef_z, coef_f, tops,
    sx, rx, sring, rring, sh, rh, sgz, rgz, sgy, rgy, scz, rcz, scf, rcf, stp, rtp,
):
    nz, ny, nf = dims
    nx = nf // CORES
    leaves = nz * ny
    rows = leaf_ref.shape[1]
    feats = raw_ref.shape[0]
    slots = elect_ref.shape[0]
    group = rows // nf
    row_pos = lax.axis_index("rows")
    f = lax.axis_index("feat")
    z, y = row_pos // ny, row_pos % ny
    x, core = f // CORES, f % CORES

    def at_z(k):
        return (lax.rem(z + k + nz, nz) * ny + y, f)

    def at_y(k):
        return (z * ny + lax.rem(y + k + ny, ny), f)

    def at_f(k):
        return (row_pos, lax.rem(f + k + nf, nf))

    started = []

    def send(src, dst, sems, dev):
        copy = pltpu.make_async_remote_copy(
            src_ref=src, dst_ref=dst, send_sem=sems[0].at[sems[2]], recv_sem=sems[1].at[sems[2]],
            device_id=dev, device_id_type=MESH,
        )
        copy.start()
        started.append(copy)

    def arrive(dst, sems):
        pltpu.make_async_remote_copy(
            src_ref=dst, dst_ref=dst, send_sem=sems[0].at[sems[2]], recv_sem=sems[1].at[sems[2]],
            device_id=(row_pos, f), device_id_type=MESH,
        ).wait_recv()

    pairs = (
        (raw_hbm, raw_ref), (leaf_hbm, leaf_ref), (elect_hbm, elect_ref), (bins_hbm, bins_ref),
        (grad_hbm, grad_ref), (hess_hbm, hess_ref), (prior_hbm, prior_ref),
    )
    loads = [pltpu.make_async_copy(a, b, load_sem.at[i]) for i, (a, b) in enumerate(pairs)]
    for load in loads:
        load.start()

    barrier = pltpu.get_barrier_semaphore()
    for k in range(1, nf):
        pl.semaphore_signal(barrier, inc=1, device_id=at_f(k), device_id_type=MESH)
    for k in range(1, nz):
        pl.semaphore_signal(barrier, inc=1, device_id=at_z(k), device_id_type=MESH)
    for k in range(1, ny):
        pl.semaphore_signal(barrier, inc=1, device_id=at_y(k), device_id_type=MESH)

    loads[0].wait()
    xt[f] = raw_ref[...].astype(F32)
    pl.semaphore_wait(barrier, (nf - 1) + (nz - 1) + (ny - 1))
    mate = (row_pos, x * CORES + (1 - core))
    for d in range(1, nx):
        dev = (row_pos, lax.rem(x + d, nx) * CORES + core)
        send(xt.at[f], xt.at[f], (sx, rx, (d - 1,)), dev)
    send(xt.at[f], xt.at[f], (sx, rx, (nx - 1,)), mate)

    for load in loads[1:]:
        load.wait()
    leaf = leaf_ref[...]
    grad = grad_ref[...].astype(BF16).astype(F32)
    hess = hess_ref[...].astype(BF16).astype(F32)
    table = elect_ref[...].astype(F32).astype(BF16)
    member = (iota((leaves, rows), 0) == leaf).astype(F32).astype(BF16)
    picked = dot(table, member, NN).astype(jnp.int32)
    bins = bins_ref[...]
    number = iota(bins.shape, 0)
    for e in range(slots):
        row = jnp.where(number == picked[e : e + 1, :], bins, 0)
        chosen[e : e + 1, :] = jnp.sum(row, axis=0, keepdims=True).astype(F32)

    def weigh(d, carry):
        first = leaf == d * ny + iota((ny, rows), 0)
        both = [jnp.where(first, grad, 0.0), jnp.where(first, hess, 0.0)]
        at = pl.multiple_of(d * (2 * ny), 2 * ny)
        wmat[0, pl.ds(at, 2 * ny), :] = jnp.concatenate(both, axis=0).astype(BF16)
        return carry

    lax.fori_loop(0, nz, weigh, 0)

    def weigh_y(d, carry):
        first = leaf == iota((nz, rows), 0) * ny + d
        both = [jnp.where(first, grad, 0.0), jnp.where(first, hess, 0.0)]
        at = pl.multiple_of(d * (2 * nz), 2 * nz)
        wmat[1, pl.ds(at, 2 * nz), :] = jnp.concatenate(both, axis=0).astype(BF16)
        return carry

    one, zero = jnp.ones((), BF16), jnp.zeros((), BF16)

    def count(e, carry):
        row = chosen[pl.ds(e, 1), :]
        number = iota((BINS, rows), 0).astype(F32).astype(BF16)
        onehot = jnp.where(number == row.astype(BF16), one, zero)
        hist[e] = dot(wmat[e // HALF], onehot, NT)
        return carry

    axes = ((nz, z, at_z, 2 * ny), (ny, y, at_y, 2 * nz))

    def piece(h, part, dest, tall):
        at = pl.multiple_of(dest * tall, tall)
        return hist.at[pl.ds(h * HALF + part * 2, 2), pl.ds(at, tall), :]

    def ring_step(s, halves=(0, 1)):
        for h in halves:
            n, me, peer, tall = axes[h]
            far = n // 2
            if s > far:
                continue
            dist = far + 1 - s
            for way, sign in enumerate((1, -1)):
                dest = lax.rem(me + sign * dist + n, n)
                for part in range(2):
                    most = far if part == way else far - 1
                    if dist > most:
                        continue
                    src = piece(h, part, dest, tall)
                    if dist < most:
                        held = ring.at[h, way, part, s - 2]
                        arrive(held, (sring, rring, (h, way, part, s - 2)))
                        held[...] += src[...]
                        src = held
                    at = (h, way, part, s - 1)
                    send(src, ring.at[at], (sring, rring, at), peer(sign))

    lax.fori_loop(0, HALF, count, 0)
    ring_step(1, (0,))
    lax.fori_loop(0, ny, weigh_y, 0)
    lax.fori_loop(HALF, slots, count, 0)
    ring_step(1, (1,))

    for d in range(1, nx):
        at = lax.rem(x - d + nx, nx) * CORES + core
        arrive(xt.at[at], (sx, rx, (d - 1,)))
        send(xt.at[at], xt.at[at], (sx, rx, (nx - 1 + d,)), mate)
    steps = max(nz, ny) // 2
    ring_step(2, (0,))
    arrive(xt.at[f], (sx, rx, (nx - 1,)))
    for d in range(1, nx):
        at = lax.rem(x - d + nx, nx) * CORES + (1 - core)
        arrive(xt.at[at], (sx, rx, (nx - 1 + d,)))
    for b in range(nf):
        block = xt[b]
        cut = pl.ds(b * group, group)
        cut2 = pl.ds(rows + b * group, group)
        scaled = hess_ref[:, cut] * block
        xb[:, cut] = block.astype(BF16)
        xb[:, cut2] = scaled.astype(BF16)
        for lz in range(nz):
            mine = leaf_ref[:, cut] == lz * ny + f
            lhs[lz * feats : (lz + 1) * feats, cut] = jnp.where(mine, scaled, 0.0).astype(BF16)
            lhs[lz * feats : (lz + 1) * feats, cut2] = jnp.where(mine, block, 0.0).astype(BF16)
    mine = leaf == iota((nz, rows), 0) * ny + f
    side_h = jnp.where(mine, hess, 0.0)
    side_g = jnp.where(mine, grad, 0.0)
    sides = jnp.concatenate([side_h, side_g], axis=0).astype(BF16)
    ones = jnp.concatenate([jnp.where(mine, 1.0, 0.0), jnp.zeros((nz, rows), F32)], axis=0)
    side = dot(sides, xb[:, 0:rows], NT) + dot(ones.astype(BF16), xb[:, rows : 2 * rows], NT)
    sum_h = jnp.sum(side_h, axis=1, keepdims=True)
    sum_g = jnp.sum(side_g, axis=1, keepdims=True)
    main = dot(lhs[...], xb[...], NT)
    fold = feats // 2
    quarter = fold // 2
    low_half = iota((fold, feats), 0) >= iota((fold, feats), 1) + 1
    on_diag = iota((fold, feats), 0) == iota((fold, feats), 1)
    lane = iota((1, LANES), 1)
    for lz in range(nz):
        block = main[lz * feats : (lz + 1) * feats, :]
        corner = jnp.concatenate([block[fold:, fold:], block[fold:, :fold]], axis=1)
        tri = jnp.where(low_half, corner, block[:fold])
        diag = jnp.sum(jnp.where(on_diag, corner, 0.0), axis=0, keepdims=True)
        parts[lz, 0:quarter, :] = jnp.concatenate([tri[:quarter], tri[quarter:]], axis=1)
        parts[lz, quarter : quarter + 1, :] = jnp.concatenate(
            [side[lz : lz + 1, :], side[nz + lz : nz + lz + 1, :]], axis=1
        )
        ends = jnp.where(lane == feats, sum_h[lz : lz + 1], 0.0)
        ends = jnp.where(lane == feats + 1, sum_g[lz : lz + 1], ends)
        parts[lz, quarter + 1 : quarter + 2, :] = ends
        parts[lz, quarter + 1 : quarter + 2, 0:feats] = diag
        parts[lz, quarter + 2 : quarter + 8, :] = jnp.zeros((6, LANES), F32)
    for k in range(1, nz):
        to = lax.rem(z + k, nz)
        send(parts.at[to], gram_z.at[k - 1], (sgz, rgz, (k - 1,)), at_z(k))

    ring_step(2, (1,))
    for s in range(3, steps):
        ring_step(s)

    total = parts[z]
    for k in range(1, nz):
        arrive(gram_z.at[k - 1], (sgz, rgz, (k - 1,)))
        total = total + gram_z[k - 1]
    gram_send[...] = total
    for k in range(1, ny):
        send(gram_send, gram_y.at[k - 1], (sgy, rgy, (k - 1,)), at_y(k))

    if steps > 2:
        ring_step(steps)

    for h, (n, me, peer, tall) in enumerate(axes):
        other, peer2 = (ny, at_y) if h == 0 else (nz, at_z)
        for part in range(2):
            out = piece(h, part, me, tall)[...]
            for way in range(2):
                far = n // 2 if part == way else n // 2 - 1
                if far > 0:
                    at = (h, way, part, n // 2 - 1)
                    arrive(ring.at[at], (sring, rring, at))
                    out = out + ring[at]
            for j in range(2):
                for gh in range(2):
                    slot = gh * HALF + part * 2 + j
                    for d in range(other):
                        spread[h, d, slot : slot + 1, :] = out[j, gh * other + d : gh * other + d + 1, :]
        here = y if h == 0 else z
        for k in range(1, other):
            to = lax.rem(here + k, other)
            send(spread.at[h, to], gathered.at[h, k - 1], (sh, rh, (h, k - 1)), peer2(k))

    for k in range(1, ny):
        arrive(gram_y.at[k - 1], (sgy, rgy, (k - 1,)))
        total = total + gram_y[k - 1]
    subs = iota((fold, LANES), 0)
    lanes = iota((fold, LANES), 1)
    turned = pltpu.roll(total[0:quarter], LANES - feats, 1)
    tri = jnp.concatenate([total[0:quarter], turned], axis=0)
    ends = total[quarter + 1 : quarter + 2]
    square[...] = jnp.zeros((LANES, LANES), F32)
    square[0:fold, :] = jnp.where(
        (lanes > subs) & (lanes < feats), tri, jnp.where(lanes == subs, 0.5 * tri, 0.0)
    )
    shifted = pltpu.roll(tri, fold, 1)
    far_diag = jnp.broadcast_to(pltpu.roll(ends, fold, 1), (fold, LANES))
    square[fold:feats, :] = jnp.where(
        (lanes >= fold) & (lanes < subs + fold), shifted,
        jnp.where(lanes == subs + fold, 0.5 * far_diag, 0.0),
    )
    edge = total[quarter : quarter + 1]
    square[feats : feats + 1, :] = jnp.where(lane < feats, edge, 0.0)
    square[feats + 1 : feats + 2, :] = jnp.where(
        lane < feats, pltpu.roll(edge, LANES - feats, 1), 0.0
    )
    square_t = square[...] + jnp.transpose(square[...])
    a = square_t[0:feats]
    lanes = iota((feats, LANES), 1)
    subs = iota((feats, LANES), 0)
    a = jnp.where(lanes <= feats, 0.5 * a, a) + jnp.where(lanes == subs, RIDGE_REG, 0.0)
    border = jnp.broadcast_to(a[:, feats : feats + 1], (feats, LANES))
    for k in range(0, feats, 2):
        c0 = jnp.broadcast_to(a[:, k : k + 1], (feats, LANES))
        c1 = jnp.broadcast_to(a[:, k + 1 : k + 2], (feats, LANES))
        r0, r1 = a[k : k + 1], a[k + 1 : k + 2]
        p00, p10 = c0[k : k + 1], c0[k + 1 : k + 2]
        p01, p11 = c1[k : k + 1], c1[k + 1 : k + 2]
        scale = 1.0 / (p00 * p11 - p01 * p10)
        n0 = (p11 * r0 - p01 * r1) * scale
        n1 = (p00 * r1 - p10 * r0) * scale
        a = a - c0 * n0 - c1 * n1
        a = jnp.where(subs == k, n0, jnp.where(subs == k + 1, n1, a))
    yc = jnp.broadcast_to(a[:, feats : feats + 1], (feats, LANES))
    yb = jnp.broadcast_to(a[:, feats + 1 : feats + 2], (feats, LANES))
    low = ends[:, feats : feats + 1] + RIDGE_REG - jnp.sum(border * yc, axis=0, keepdims=True)
    high = ends[:, feats + 1 : feats + 2] - jnp.sum(border * yb, axis=0, keepdims=True)
    const = high / low
    answer = jnp.sum(jnp.where(lanes == subs, yb - const * yc, 0.0), axis=0, keepdims=True)
    coef_z[z] = -jnp.where(lane == feats, const, answer)
    for k in range(1, nz):
        send(coef_z.at[z], coef_z.at[z], (scz, rcz, (k - 1,)), at_z(k))

    upper = (iota((BINS, BINS), 0) <= iota((BINS, BINS), 1)).astype(F32).astype(BF16)
    gains = []
    for h in range(2):
        other = ny if h == 0 else nz
        sums = spread[h, y if h == 0 else z]
        for k in range(1, other):
            arrive(gathered.at[h, k - 1], (sh, rh, (h, k - 1)))
            sums = sums + gathered[h, k - 1]
        hi, mid, lo = split3(sums)
        run = dot(hi, upper, NN) + dot(mid, upper, NN) + dot(lo, upper, NN)
        lg, lh = run[0:HALF], run[HALF : 2 * HALF]
        tg, th = lg[:, BINS - 1 : BINS], lh[:, BINS - 1 : BINS]
        rg = tg - lg
        gains.append(
            lg * lg / (lh + SPLIT_REG) + rg * rg / (th - lh + SPLIT_REG) - tg * tg / (th + SPLIT_REG)
        )
    top = jnp.maximum(gains[0], gains[1])
    top = jnp.max(jnp.max(top, axis=1, keepdims=True), axis=0, keepdims=True)
    tops[f] = jnp.broadcast_to(top, (8, LANES))
    for k in range(1, nf):
        send(tops.at[f], tops.at[f], (stp, rtp, (k - 1,)), at_f(k))

    for k in range(1, nz):
        at = lax.rem(z - k + nz, nz)
        arrive(coef_z.at[at], (scz, rcz, (k - 1,)))
    for k in range(nz):
        coef_f[f, k : k + 1, :] = coef_z[k]
    for k in range(1, nf):
        send(coef_f.at[f], coef_f.at[f], (scf, rcf, (k - 1,)), at_f(k))

    for k in range(1, nf):
        at = lax.rem(f - k + nf, nf)
        arrive(tops.at[at], (stp, rtp, (k - 1,)))
    best = tops[0]
    for k in range(1, nf):
        best = jnp.maximum(best, tops[k])
    best = best[0:1, 0:1]
    for h in range(2):
        gain_ref[0, h * HALF : (h + 1) * HALF, :] = gains[h] - best

    for k in range(1, nf):
        at = lax.rem(f - k + nf, nf)
        arrive(coef_f.at[at], (scf, rcf, (k - 1,)))
    coef_ref[...] = coef_f[y, pl.ds(z, 1), 0 : feats + 1]
    own = leaf_ref[:, pl.ds(pl.multiple_of(f * group, group), group)]
    tables = jnp.concatenate([coef_f[k] for k in range(nf)], axis=0)
    if leaves < LANES:
        tables = jnp.concatenate([tables, jnp.zeros((LANES - leaves, LANES), F32)], axis=0)
    column = jnp.transpose(tables)
    key = lax.rem(own, ny) * nz + own // ny
    pick = (iota((LANES, group), 0) == key).astype(F32).astype(BF16)
    hi, mid, lo = split3(column)
    per_row = dot(hi, pick, NN) + dot(mid, pick, NN) + dot(lo, pick, NN)
    value = jnp.sum(xt[f] * per_row[0:feats], axis=0, keepdims=True) + per_row[feats : feats + 1]
    score_ref[...] = prior_ref[...] + SHRINKAGE * value

    for copy in started:
        copy.wait_send()


def body(bin_ids, leaf_ids, gradient, hessian, raw_feats, prior_score, elected):
    rows = bin_ids.shape[1]
    leaves, slots = elected.shape
    nf = lax.axis_size("feat")
    ny = nf
    nz = lax.axis_size("rows") // ny
    group, feats = raw_feats.shape
    small = lambda width, kind: pltpu.VMEM((1, width), kind)
    nx = nf // CORES
    far = max(nz, ny)
    tall = 2 * ny
    dma = pltpu.SemaphoreType.DMA
    vmem = pltpu.VMEM
    scratch = [
        vmem((bin_ids.shape[0], rows), jnp.int32),
        small(rows, jnp.int32), small(rows, F32), small(rows, F32),
        vmem((feats, group), BF16), small(group, F32), vmem((slots, leaves), jnp.int32), dma((7,)),
        vmem((nf, feats, group), F32),
        vmem((slots, rows), F32),
        vmem((2, 2 * leaves, rows), BF16),
        vmem((slots, 2 * leaves, BINS), F32),
        vmem((2, 2, 2, far // 2, 2, tall, BINS), F32),
        vmem((2, far, 2 * HALF, BINS), F32),
        vmem((2, far - 1, 2 * HALF, BINS), F32),
        vmem((feats, 2 * rows), BF16),
        vmem((nz * feats, 2 * rows), BF16),
        vmem((nz, PACK, LANES), F32),
        vmem((nz - 1, PACK, LANES), F32),
        vmem((PACK, LANES), F32),
        vmem((ny - 1, PACK, LANES), F32),
        vmem((LANES, LANES), F32),
        vmem((nz, 1, LANES), F32),
        vmem((nf, nz, LANES), F32),
        vmem((nf, 8, LANES), F32),
    ]
    counts = [
        (2 * nx - 1,), (2, 2, 2, far // 2), (2, far - 1), (nz - 1,), (ny - 1,), (nz - 1,),
        (nf - 1,), (nf - 1,),
    ]
    for shape in counts:
        scratch += [dma(shape), dma(shape)]
    gain, coef, score = pl.pallas_call(
        functools.partial(kernel, (nz, ny, nf)),
        out_shape=(
            jax.ShapeDtypeStruct((1, slots, BINS), F32),
            jax.ShapeDtypeStruct((1, feats + 1), F32),
            jax.ShapeDtypeStruct((1, group), F32),
        ),
        in_specs=[pl.BlockSpec(memory_space=pltpu.HBM)] * 7,
        out_specs=(pl.BlockSpec(memory_space=pltpu.VMEM),) * 3,
        scratch_shapes=scratch,
        compiler_params=pltpu.CompilerParams(
            collective_id=0, has_side_effects=True, vmem_limit_bytes=66_000_000
        ),
        name="level",
    )(
        bin_ids, leaf_ids.reshape(1, rows), gradient.reshape(1, rows), hessian.reshape(1, rows),
        raw_feats.T, prior_score.reshape(1, group), elected.T,
    )
    return gain, coef, score.reshape(group)


def solution(mesh):
    in_specs = (
        P("feat", "rows"),
        P("rows"),
        P("rows"),
        P("rows"),
        P(("rows", "feat"), None),
        P(("rows", "feat")),
        P(None, "feat"),
    )
    out_specs = (P("rows", "feat", None), P("rows", None), P(("rows", "feat")))
    return jax.shard_map(body, mesh=mesh, in_specs=in_specs, out_specs=out_specs, check_vma=False)
```

```python
import functools

import jax
import jax.numpy as jnp
from jax import lax
from jax.experimental import pallas as pl
from jax.experimental.pallas import tpu as pltpu
from jax.sharding import PartitionSpec as P

BINS = 256
CORES = 2
HALF = 4
PACK = 24
SUB = 16
LANES = 128
SPLIT_REG = 1.0
RIDGE_REG = 1.0
SHRINKAGE = 0.3
MESH = pl.DeviceIdType.MESH
NT = (((1,), (1,)), ((), ()))
NN = (((1,), (0,)), ((), ()))
F32 = jnp.float32
BF16 = jnp.bfloat16


def dot(a, b, dims):
    return lax.dot_general(a, b, dims, preferred_element_type=F32)


def iota(shape, axis):
    return lax.broadcasted_iota(jnp.int32, shape, axis)


def split3(v):
    hi = v.astype(BF16)
    rest = v - hi.astype(F32)
    mid = rest.astype(BF16)
    return hi, mid, (rest - mid.astype(F32)).astype(BF16)


def kernel(
    dims, bins_hbm, leaf_hbm, grad_hbm, hess_hbm, raw_hbm, prior_hbm, elect_hbm,
    gain_ref, coef_ref, score_ref,
    bins_ref, leaf_ref, grad_ref, hess_ref, raw_ref, prior_ref, elect_ref, load_sem, entered,
    xt, sifted, chosen, wmat, hist, ring, spread, gathered, xb,
    parts, gram_z, gram_send, gram_y, square, coef_z, tops,
    sx, rx, sring, rring, sh, rh, sgz, rgz, sgy, rgy, scz, rcz, stp, rtp,
):
    nz, ny, nf = dims
    nx = nf // CORES
    leaves = nz * ny
    rows = leaf_ref.shape[1]
    feats = raw_ref.shape[0]
    slots = elect_ref.shape[0]
    group = rows // nf
    row_pos = lax.axis_index("rows")
    f = lax.axis_index("feat")
    z, y = row_pos // ny, row_pos % ny
    x, core = f // CORES, f % CORES

    def at_z(k):
        return (lax.rem(z + k + nz, nz) * ny + y, f)

    def at_y(k):
        return (z * ny + lax.rem(y + k + ny, ny), f)

    def at_f(k):
        return (row_pos, lax.rem(f + k + nf, nf))

    started = []

    def send(src, dst, sems, dev):
        copy = pltpu.make_async_remote_copy(
            src_ref=src, dst_ref=dst, send_sem=sems[0].at[sems[2]], recv_sem=sems[1].at[sems[2]],
            device_id=dev, device_id_type=MESH,
        )
        copy.start()
        started.append(copy)

    def arrive(dst, sems):
        pltpu.make_async_remote_copy(
            src_ref=dst, dst_ref=dst, send_sem=sems[0].at[sems[2]], recv_sem=sems[1].at[sems[2]],
            device_id=(row_pos, f), device_id_type=MESH,
        ).wait_recv()

    pairs = (
        (raw_hbm, raw_ref), (leaf_hbm, leaf_ref), (elect_hbm, elect_ref), (bins_hbm, bins_ref),
        (grad_hbm, grad_ref), (hess_hbm, hess_ref), (prior_hbm, prior_ref),
    )
    loads = [pltpu.make_async_copy(a, b, load_sem.at[i]) for i, (a, b) in enumerate(pairs)]
    for load in loads:
        load.start()

    barrier = pltpu.get_barrier_semaphore()
    beside = (at_z(1), at_z(-1), at_y(1), at_y(-1))
    for dev in beside:
        pl.semaphore_signal(barrier, inc=1, device_id=dev, device_id_type=MESH)
    for k in range(1, nf):
        pl.semaphore_signal(barrier, inc=1, device_id=at_f(k), device_id_type=MESH)

    rounds = max(nz, ny) // 2 - 1

    def heard(r):
        if 0 <= r < rounds:
            for i in range(2):
                pl.semaphore_wait(entered.at[r, i], 2)

    def pass_on(r):
        heard(r - 1)
        if r < rounds:
            for i, dev in enumerate(beside):
                pl.semaphore_signal(entered.at[r, i // 2], inc=1, device_id=dev, device_id_type=MESH)

    loads[0].wait()
    xt[f] = raw_ref[...].astype(F32)
    pl.semaphore_wait(barrier, (nf - 1) + len(beside))
    mate = (row_pos, x * CORES + (1 - core))
    for d in range(1, nx):
        dev = (row_pos, lax.rem(x + d, nx) * CORES + core)
        send(xt.at[f], xt.at[f], (sx, rx, (d - 1,)), dev)
    send(xt.at[f], xt.at[f], (sx, rx, (nx - 1,)), mate)

    pass_on(0)

    for load in loads[1:]:
        load.wait()
    leaf = leaf_ref[...]
    grad = grad_ref[...].astype(BF16).astype(F32)
    hess = hess_ref[...].astype(BF16).astype(F32)
    table = elect_ref[...].astype(F32).astype(BF16)
    member = (iota((leaves, rows), 0) == leaf).astype(F32).astype(BF16)
    picked = dot(table, member, NN)
    one, zero = jnp.ones((), BF16), jnp.zeros((), BF16)
    bins = bins_ref[...].astype(F32).astype(BF16)
    ahead = iota((SUB, rows), 0)
    for e in range(slots):
        row = picked[e : e + 1, :].astype(BF16)
        held = zero
        for g in range(bins.shape[0] // SUB):
            number = (ahead + g * SUB).astype(F32).astype(BF16)
            held = jnp.where(number == row, bins[g * SUB : (g + 1) * SUB], held)
        sifted[e * SUB : (e + 1) * SUB, :] = held
    gather_rows = iota((slots, slots * SUB), 1) // SUB == iota((slots, slots * SUB), 0)
    chosen[...] = dot(gather_rows.astype(F32).astype(BF16), sifted[...], NN)

    def weigh(d, carry):
        first = leaf == d * ny + iota((ny, rows), 0)
        both = [jnp.where(first, grad, 0.0), jnp.where(first, hess, 0.0)]
        at = pl.multiple_of(d * (2 * ny), 2 * ny)
        wmat[0, pl.ds(at, 2 * ny), :] = jnp.concatenate(both, axis=0).astype(BF16)
        return carry

    lax.fori_loop(0, nz, weigh, 0)

    def weigh_y(d, carry):
        first = leaf == iota((nz, rows), 0) * ny + d
        both = [jnp.where(first, grad, 0.0), jnp.where(first, hess, 0.0)]
        at = pl.multiple_of(d * (2 * nz), 2 * nz)
        wmat[1, pl.ds(at, 2 * nz), :] = jnp.concatenate(both, axis=0).astype(BF16)
        return carry

    def count(e, carry):
        row = chosen[pl.ds(e, 1), :]
        number = iota((BINS, rows), 0).astype(F32).astype(BF16)
        onehot = jnp.where(number == row.astype(BF16), one, zero)
        hist[e] = dot(wmat[e // HALF], onehot, NT)
        return carry

    axes = ((nz, z, at_z, 2 * ny), (ny, y, at_y, 2 * nz))

    def piece(h, part, dest, tall):
        at = pl.multiple_of(dest * tall, tall)
        return hist.at[pl.ds(h * HALF + part * 2, 2), pl.ds(at, tall), :]

    def ring_step(s, halves=(0, 1)):
        for h in halves:
            n, me, peer, tall = axes[h]
            far = n // 2
            if s > far:
                continue
            dist = far + 1 - s
            for way, sign in enumerate((1, -1)):
                dest = lax.rem(me + sign * dist + n, n)
                for part in range(2):
                    most = far if part == way else far - 1
                    if dist > most:
                        continue
                    src = piece(h, part, dest, tall)
                    if dist < most:
                        held = ring.at[h, way, part, s - 2]
                        arrive(held, (sring, rring, (h, way, part, s - 2)))
                        held[...] += src[...]
                        src = held
                    at = (h, way, part, s - 1)
                    send(src, ring.at[at], (sring, rring, at), peer(sign))

    lax.fori_loop(0, HALF, count, 0)
    ring_step(1, (0,))
    pass_on(1)
    lax.fori_loop(0, ny, weigh_y, 0)
    lax.fori_loop(HALF, slots, count, 0)
    ring_step(1, (1,))
    pass_on(2)

    parts[...] = jnp.zeros_like(parts)
    edge = iota((SUB, rows), 0)
    xb[feats : feats + SUB, 0:rows] = jnp.where(edge == 0, 1.0, 0.0).astype(BF16)
    xb[feats : feats + SUB, rows : 2 * rows] = jnp.where(
        edge == 0, hess, jnp.where(edge == 1, grad, 0.0)
    ).astype(BF16)
    in_leaf = [jnp.where(leaf == lz * ny + f, 1.0, 0.0).astype(BF16) for lz in range(nz)]
    mine = leaf == iota((nz, rows), 0) * ny + f
    sum_h = jnp.sum(jnp.where(mine, hess, 0.0), axis=1, keepdims=True)
    sum_g = jnp.sum(jnp.where(mine, grad, 0.0), axis=1, keepdims=True)
    at_lane = iota((nz, LANES), 1)
    ends = jnp.where(at_lane == feats, sum_h, jnp.where(at_lane == feats + 1, sum_g, 0.0))

    for d in range(1, nx):
        at = lax.rem(x - d + nx, nx) * CORES + core
        arrive(xt.at[at], (sx, rx, (d - 1,)))
        send(xt.at[at], xt.at[at], (sx, rx, (nx - 1 + d,)), mate)
    steps = max(nz, ny) // 2
    ring_step(2, (0,))
    arrive(xt.at[f], (sx, rx, (nx - 1,)))
    for d in range(1, nx):
        at = lax.rem(x - d + nx, nx) * CORES + (1 - core)
        arrive(xt.at[at], (sx, rx, (nx - 1 + d,)))
    for b in range(nf):
        block = xt[b]
        cut = pl.ds(b * group, group)
        cut2 = pl.ds(rows + b * group, group)
        scaled = hess_ref[:, cut] * block
        xb[0:feats, cut] = block.astype(BF16)
        xb[0:feats, cut2] = scaled.astype(BF16)
    right = [jnp.concatenate([xb[0:feats, rows:] * m, xb[0:feats, :rows] * m], axis=1) for m in in_leaf]
    wide = dot(xb[...], jnp.concatenate(right, axis=0), NT)
    fold = feats // 2
    quarter = fold // 2
    span = (fold, nz * feats)
    behind = lax.rem(iota(span, 1), feats) - iota(span, 0)
    corner = pltpu.roll(wide[fold:feats], nz * feats - fold, 1)
    tri = jnp.where(behind < 0, corner, wide[0:fold])
    diag = jnp.sum(jnp.where(behind == 0, corner, 0.0), axis=0, keepdims=True)
    first = iota((1, LANES), 1) < feats
    lane = iota((1, LANES), 1)
    for t in range(nz // 2):
        cut = slice(t * LANES, (t + 1) * LANES)
        upper, lower = tri[0:quarter, cut], tri[quarter:fold, cut]
        edge = wide[feats : feats + 8, cut]
        turned = pltpu.roll(edge, feats, 1)
        even, odd = 2 * t, 2 * t + 1
        parts[even, 0:quarter, :] = jnp.where(first, upper, pltpu.roll(lower, feats, 1))
        parts[odd, 0:quarter, :] = jnp.where(first, pltpu.roll(upper, feats, 1), lower)
        parts[even, quarter : quarter + 1, :] = jnp.where(first, edge[0:1], turned[1:2])
        parts[odd, quarter : quarter + 1, :] = jnp.where(first, turned[0:1], edge[1:2])
        here = diag[:, cut]
        for lz, row in ((even, here), (odd, pltpu.roll(here, feats, 1))):
            parts[lz, quarter + 1 : quarter + 2, :] = jnp.where(first, row, ends[lz : lz + 1])
    heard(2)
    for k in range(1, nz):
        to = lax.rem(z + k, nz)
        send(parts.at[to], gram_z.at[k - 1], (sgz, rgz, (k - 1,)), at_z(k))

    ring_step(2, (1,))
    for s in range(3, steps):
        ring_step(s)

    total = parts[z]
    for k in range(1, nz):
        arrive(gram_z.at[k - 1], (sgz, rgz, (k - 1,)))
        total = total + gram_z[k - 1]
    gram_send[...] = total
    for k in range(1, ny):
        send(gram_send, gram_y.at[k - 1], (sgy, rgy, (k - 1,)), at_y(k))

    if steps > 2:
        ring_step(steps)

    for h, (n, me, peer, tall) in enumerate(axes):
        other, peer2 = (ny, at_y) if h == 0 else (nz, at_z)
        for part in range(2):
            out = piece(h, part, me, tall)[...]
            for way in range(2):
                far = n // 2 if part == way else n // 2 - 1
                if far > 0:
                    at = (h, way, part, n // 2 - 1)
                    arrive(ring.at[at], (sring, rring, at))
                    out = out + ring[at]
            for j in range(2):
                for gh in range(2):
                    slot = gh * HALF + part * 2 + j
                    for d in range(other):
                        spread[h, d, slot : slot + 1, :] = out[j, gh * other + d : gh * other + d + 1, :]
        here = y if h == 0 else z
        for k in range(1, other):
            to = lax.rem(here + k, other)
            send(spread.at[h, to], gathered.at[h, k - 1], (sh, rh, (h, k - 1)), peer2(k))

    for k in range(1, ny):
        arrive(gram_y.at[k - 1], (sgy, rgy, (k - 1,)))
        total = total + gram_y[k - 1]
    subs = iota((fold, LANES), 0)
    lanes = iota((fold, LANES), 1)
    turned = pltpu.roll(total[0:quarter], LANES - feats, 1)
    tri = jnp.concatenate([total[0:quarter], turned], axis=0)
    ends = total[quarter + 1 : quarter + 2]
    square[...] = jnp.zeros((LANES, LANES), F32)
    square[0:fold, :] = jnp.where(
        (lanes > subs) & (lanes < feats), tri, jnp.where(lanes == subs, 0.5 * tri, 0.0)
    )
    shifted = pltpu.roll(tri, fold, 1)
    far_diag = jnp.broadcast_to(pltpu.roll(ends, fold, 1), (fold, LANES))
    square[fold:feats, :] = jnp.where(
        (lanes >= fold) & (lanes < subs + fold), shifted,
        jnp.where(lanes == subs + fold, 0.5 * far_diag, 0.0),
    )
    edge = total[quarter : quarter + 1]
    square[feats : feats + 1, :] = jnp.where(lane < feats, edge, 0.0)
    square[feats + 1 : feats + 2, :] = jnp.where(
        lane < feats, pltpu.roll(edge, LANES - feats, 1), 0.0
    )
    square_t = square[...] + jnp.transpose(square[...])
    a = square_t[0:feats]
    lanes = iota((feats, LANES), 1)
    subs = iota((feats, LANES), 0)
    a = jnp.where(lanes <= feats, 0.5 * a, a) + jnp.where(lanes == subs, RIDGE_REG, 0.0)
    border = jnp.broadcast_to(a[:, feats : feats + 1], (feats, LANES))
    for k in range(0, feats, 2):
        c0 = jnp.broadcast_to(a[:, k : k + 1], (feats, LANES))
        c1 = jnp.broadcast_to(a[:, k + 1 : k + 2], (feats, LANES))
        r0, r1 = a[k : k + 1], a[k + 1 : k + 2]
        p00, p10 = c0[k : k + 1], c0[k + 1 : k + 2]
        p01, p11 = c1[k : k + 1], c1[k + 1 : k + 2]
        scale = 1.0 / (p00 * p11 - p01 * p10)
        n0 = (p11 * r0 - p01 * r1) * scale
        n1 = (p00 * r1 - p10 * r0) * scale
        a = a - c0 * n0 - c1 * n1
        a = jnp.where(subs == k, n0, jnp.where(subs == k + 1, n1, a))
    yc = jnp.broadcast_to(a[:, feats : feats + 1], (feats, LANES))
    yb = jnp.broadcast_to(a[:, feats + 1 : feats + 2], (feats, LANES))
    low = ends[:, feats : feats + 1] + RIDGE_REG - jnp.sum(border * yc, axis=0, keepdims=True)
    high = ends[:, feats + 1 : feats + 2] - jnp.sum(border * yb, axis=0, keepdims=True)
    const = high / low
    answer = jnp.sum(jnp.where(lanes == subs, yb - const * yc, 0.0), axis=0, keepdims=True)
    early = list(started)
    started.clear()
    own = f * nz + z
    coef_z[own] = -jnp.where(lane == feats, const, answer)

    def give(k, carry):
        dz = lax.rem(lax.div(k, nf) + nz // 2, nz)
        df = lax.rem(lax.rem(k, nf) + nf // 2, nf)

        @pl.when(dz + df > 0)
        def _():
            dev = (lax.rem(z + dz, nz) * ny + y, lax.rem(f + df, nf))
            pltpu.make_async_remote_copy(
                src_ref=coef_z.at[own], dst_ref=coef_z.at[own], send_sem=scz.at[0], recv_sem=rcz.at[0],
                device_id=dev, device_id_type=MESH,
            ).start()

        return carry

    lax.fori_loop(0, nz * nf, give, 0)
    shared = pltpu.make_async_remote_copy(
        src_ref=coef_z.at[pl.ds(0, nz * nf - 1)], dst_ref=coef_z.at[pl.ds(0, nz * nf - 1)],
        send_sem=scz.at[0], recv_sem=rcz.at[0], device_id=(row_pos, f), device_id_type=MESH,
    )

    upper = (iota((BINS, BINS), 0) <= iota((BINS, BINS), 1)).astype(F32).astype(BF16)
    gains = []
    for h in range(2):
        other = ny if h == 0 else nz
        sums = spread[h, y if h == 0 else z]
        for k in range(1, other):
            arrive(gathered.at[h, k - 1], (sh, rh, (h, k - 1)))
            sums = sums + gathered[h, k - 1]
        hi, mid, lo = split3(sums)
        run = dot(hi, upper, NN) + dot(mid, upper, NN) + dot(lo, upper, NN)
        lg, lh = run[0:HALF], run[HALF : 2 * HALF]
        tg, th = lg[:, BINS - 1 : BINS], lh[:, BINS - 1 : BINS]
        rg = tg - lg
        gains.append(
            lg * lg / (lh + SPLIT_REG) + rg * rg / (th - lh + SPLIT_REG) - tg * tg / (th + SPLIT_REG)
        )
    top = jnp.maximum(gains[0], gains[1])
    top = jnp.max(jnp.max(top, axis=1, keepdims=True), axis=0, keepdims=True)
    tops[f] = jnp.broadcast_to(top, (8, LANES))
    for k in range(1, nf):
        send(tops.at[f], tops.at[f], (stp, rtp, (k - 1,)), at_f(k))

    for copy in early:
        copy.wait_send()

    for k in range(1, nf):
        at = lax.rem(f - k + nf, nf)
        arrive(tops.at[at], (stp, rtp, (k - 1,)))
    best = tops[0]
    for k in range(1, nf):
        best = jnp.maximum(best, tops[k])
    best = best[0:1, 0:1]
    for h in range(2):
        gain_ref[0, h * HALF : (h + 1) * HALF, :] = gains[h] - best

    shared.wait_recv()
    coef_ref[...] = coef_z[y * nz + z][:, 0 : feats + 1]
    own_rows = leaf_ref[:, pl.ds(pl.multiple_of(f * group, group), group)]
    tables = jnp.concatenate([coef_z[k] for k in range(nz * nf)], axis=0)
    if leaves < LANES:
        tables = jnp.concatenate([tables, jnp.zeros((LANES - leaves, LANES), F32)], axis=0)
    column = jnp.transpose(tables)
    key = lax.rem(own_rows, ny) * nz + own_rows // ny
    pick = (iota((LANES, group), 0) == key).astype(F32).astype(BF16)
    hi, mid, lo = split3(column)
    per_row = dot(hi, pick, NN) + dot(mid, pick, NN) + dot(lo, pick, NN)
    value = jnp.sum(xt[f] * per_row[0:feats], axis=0, keepdims=True) + per_row[feats : feats + 1]
    score_ref[...] = prior_ref[...] + SHRINKAGE * value

    for copy in started:
        copy.wait_send()
    shared.wait_send()


def body(bin_ids, leaf_ids, gradient, hessian, raw_feats, prior_score, elected):
    rows = bin_ids.shape[1]
    leaves, slots = elected.shape
    nf = lax.axis_size("feat")
    ny = nf
    nz = lax.axis_size("rows") // ny
    group, feats = raw_feats.shape
    small = lambda width, kind: pltpu.VMEM((1, width), kind)
    nx = nf // CORES
    far = max(nz, ny)
    tall = 2 * ny
    dma = pltpu.SemaphoreType.DMA
    vmem = pltpu.VMEM
    scratch = [
        vmem((bin_ids.shape[0], rows), jnp.int32),
        small(rows, jnp.int32), small(rows, F32), small(rows, F32),
        vmem((feats, group), BF16), small(group, F32), vmem((slots, leaves), jnp.int32), dma((7,)),
        pltpu.SemaphoreType.REGULAR((max(nz, ny) // 2 - 1, 2)),
        vmem((nf, feats, group), F32),
        vmem((slots * SUB, rows), BF16),
        vmem((slots, rows), F32),
        vmem((2, 2 * leaves, rows), BF16),
        vmem((slots, 2 * leaves, BINS), F32),
        vmem((2, 2, 2, far // 2, 2, tall, BINS), F32),
        vmem((2, far, 2 * HALF, BINS), F32),
        vmem((2, far - 1, 2 * HALF, BINS), F32),
        vmem((feats + SUB, 2 * rows), BF16),
        vmem((nz, PACK, LANES), F32),
        vmem((nz - 1, PACK, LANES), F32),
        vmem((PACK, LANES), F32),
        vmem((ny - 1, PACK, LANES), F32),
        vmem((LANES, LANES), F32),
        vmem((nz * nf, 1, LANES), F32),
        vmem((nf, 8, LANES), F32),
    ]
    counts = [
        (2 * nx - 1,), (2, 2, 2, far // 2), (2, far - 1), (nz - 1,), (ny - 1,), (1,),
        (nf - 1,),
    ]
    for shape in counts:
        scratch += [dma(shape), dma(shape)]
    gain, coef, score = pl.pallas_call(
        functools.partial(kernel, (nz, ny, nf)),
        out_shape=(
            jax.ShapeDtypeStruct((1, slots, BINS), F32),
            jax.ShapeDtypeStruct((1, feats + 1), F32),
            jax.ShapeDtypeStruct((1, group), F32),
        ),
        in_specs=[pl.BlockSpec(memory_space=pltpu.HBM)] * 7,
        out_specs=(pl.BlockSpec(memory_space=pltpu.VMEM),) * 3,
        scratch_shapes=scratch,
        compiler_params=pltpu.CompilerParams(
            collective_id=0, has_side_effects=True, vmem_limit_bytes=66_000_000
        ),
        name="level",
    )(
        bin_ids, leaf_ids.reshape(1, rows), gradient.reshape(1, rows), hessian.reshape(1, rows),
        raw_feats.T, prior_score.reshape(1, group), elected.T,
    )
    return gain, coef, score.reshape(group)


def solution(mesh):
    in_specs = (
        P("feat", "rows"),
        P("rows"),
        P("rows"),
        P("rows"),
        P(("rows", "feat"), None),
        P(("rows", "feat")),
        P(None, "feat"),
    )
    out_specs = (P("rows", "feat", None), P("rows", None), P(("rows", "feat")))
    return jax.shard_map(body, mesh=mesh, in_specs=in_specs, out_specs=out_specs, check_vma=False)
```

```python
import functools

import jax
import jax.numpy as jnp
from jax import lax
from jax.experimental import pallas as pl
from jax.experimental.pallas import tpu as pltpu
from jax.sharding import PartitionSpec as P

BINS = 256
CORES = 2
HALF = 4
PACK = 24
SUB = 16
LANES = 128
SPLIT_REG = 1.0
RIDGE_REG = 1.0
SHRINKAGE = 0.3
MESH = pl.DeviceIdType.MESH
NT = (((1,), (1,)), ((), ()))
NN = (((1,), (0,)), ((), ()))
F32 = jnp.float32
BF16 = jnp.bfloat16


def dot(a, b, dims):
    return lax.dot_general(a, b, dims, preferred_element_type=F32)


def iota(shape, axis):
    return lax.broadcasted_iota(jnp.int32, shape, axis)


def split3(v):
    hi = v.astype(BF16)
    rest = v - hi.astype(F32)
    mid = rest.astype(BF16)
    return hi, mid, (rest - mid.astype(F32)).astype(BF16)


def kernel(
    dims, bins_hbm, leaf_hbm, grad_hbm, hess_hbm, raw_hbm, prior_hbm, elect_hbm,
    gain_ref, coef_ref, score_ref,
    bins_ref, leaf_ref, grad_ref, hess_ref, raw_ref, prior_ref, elect_ref, load_sem, entered,
    xt, sifted, chosen, wmat, hist, ring, spread, gathered, xb,
    parts, gram_z, gram_send, gram_y, square, coef_z, tops,
    sx, rx, sring, rring, sh, rh, sgz, rgz, sgy, rgy, scz, rcz, stp, rtp,
):
    nz, ny, nf = dims
    nx = nf // CORES
    leaves = nz * ny
    rows = leaf_ref.shape[1]
    feats = raw_ref.shape[0]
    slots = elect_ref.shape[0]
    group = rows // nf
    row_pos = lax.axis_index("rows")
    f = lax.axis_index("feat")
    z, y = row_pos // ny, row_pos % ny
    x, core = f // CORES, f % CORES

    def at_z(k):
        return (lax.rem(z + k + nz, nz) * ny + y, f)

    def at_y(k):
        return (z * ny + lax.rem(y + k + ny, ny), f)

    def at_f(k):
        return (row_pos, lax.rem(f + k + nf, nf))

    started = []

    def send(src, dst, sems, dev):
        copy = pltpu.make_async_remote_copy(
            src_ref=src, dst_ref=dst, send_sem=sems[0].at[sems[2]], recv_sem=sems[1].at[sems[2]],
            device_id=dev, device_id_type=MESH,
        )
        copy.start()
        started.append(copy)

    def arrive(dst, sems):
        pltpu.make_async_remote_copy(
            src_ref=dst, dst_ref=dst, send_sem=sems[0].at[sems[2]], recv_sem=sems[1].at[sems[2]],
            device_id=(row_pos, f), device_id_type=MESH,
        ).wait_recv()

    pairs = (
        (raw_hbm, raw_ref), (leaf_hbm, leaf_ref), (elect_hbm, elect_ref), (bins_hbm, bins_ref),
        (grad_hbm, grad_ref), (hess_hbm, hess_ref), (prior_hbm, prior_ref),
    )
    loads = [pltpu.make_async_copy(a, b, load_sem.at[i]) for i, (a, b) in enumerate(pairs)]
    for load in loads:
        load.start()

    barrier = pltpu.get_barrier_semaphore()
    beside = (at_z(1), at_z(-1), at_y(1), at_y(-1))
    for dev in beside:
        pl.semaphore_signal(barrier, inc=1, device_id=dev, device_id_type=MESH)
    for k in range(1, nf):
        pl.semaphore_signal(barrier, inc=1, device_id=at_f(k), device_id_type=MESH)

    rounds = max(nz, ny) // 2 - 1

    def heard(r):
        if 0 <= r < rounds:
            for i in range(2):
                pl.semaphore_wait(entered.at[r, i], 2)

    def pass_on(r):
        heard(r - 1)
        if r < rounds:
            for i, dev in enumerate(beside):
                pl.semaphore_signal(entered.at[r, i // 2], inc=1, device_id=dev, device_id_type=MESH)

    loads[0].wait()
    xt[f] = raw_ref[...].astype(F32)
    pl.semaphore_wait(barrier, (nf - 1) + len(beside))
    mate = (row_pos, x * CORES + (1 - core))
    for d in range(1, nx):
        dev = (row_pos, lax.rem(x + d, nx) * CORES + core)
        send(xt.at[f], xt.at[f], (sx, rx, (d - 1,)), dev)
    send(xt.at[f], xt.at[f], (sx, rx, (nx - 1,)), mate)

    pass_on(0)

    for load in loads[1:]:
        load.wait()
    leaf = leaf_ref[...]
    grad = grad_ref[...].astype(BF16).astype(F32)
    hess = hess_ref[...].astype(BF16).astype(F32)
    table = elect_ref[...].astype(F32).astype(BF16)
    member = (iota((leaves, rows), 0) == leaf).astype(F32).astype(BF16)
    picked = dot(table, member, NN)
    one, zero = jnp.ones((), BF16), jnp.zeros((), BF16)
    bins = bins_ref[...].astype(F32).astype(BF16)
    ahead = iota((SUB, rows), 0)
    for e in range(slots):
        row = picked[e : e + 1, :].astype(BF16)
        held = zero
        for g in range(bins.shape[0] // SUB):
            number = (ahead + g * SUB).astype(F32).astype(BF16)
            held = jnp.where(number == row, bins[g * SUB : (g + 1) * SUB], held)
        sifted[e * SUB : (e + 1) * SUB, :] = held
    gather_rows = iota((slots, slots * SUB), 1) // SUB == iota((slots, slots * SUB), 0)
    chosen[...] = dot(gather_rows.astype(F32).astype(BF16), sifted[...], NN)

    def weigh(d, carry):
        first = leaf == d * ny + iota((ny, rows), 0)
        both = [jnp.where(first, grad, 0.0), jnp.where(first, hess, 0.0)]
        at = pl.multiple_of(d * (2 * ny), 2 * ny)
        wmat[0, pl.ds(at, 2 * ny), :] = jnp.concatenate(both, axis=0).astype(BF16)
        return carry

    lax.fori_loop(0, nz, weigh, 0)

    def weigh_y(d, carry):
        first = leaf == iota((nz, rows), 0) * ny + d
        both = [jnp.where(first, grad, 0.0), jnp.where(first, hess, 0.0)]
        at = pl.multiple_of(d * (2 * nz), 2 * nz)
        wmat[1, pl.ds(at, 2 * nz), :] = jnp.concatenate(both, axis=0).astype(BF16)
        return carry

    def count(e, carry):
        row = chosen[pl.ds(e, 1), :]
        number = iota((BINS, rows), 0).astype(F32).astype(BF16)
        onehot = jnp.where(number == row.astype(BF16), one, zero)
        hist[e] = dot(wmat[e // HALF], onehot, NT)
        return carry

    axes = ((nz, z, at_z, 2 * ny), (ny, y, at_y, 2 * nz))

    def piece(h, part, dest, tall):
        at = pl.multiple_of(dest * tall, tall)
        return hist.at[pl.ds(h * HALF + part * 2, 2), pl.ds(at, tall), :]

    def ring_step(s, halves=(0, 1)):
        for h in halves:
            n, me, peer, tall = axes[h]
            far = n // 2
            if s > far:
                continue
            dist = far + 1 - s
            for way, sign in enumerate((1, -1)):
                dest = lax.rem(me + sign * dist + n, n)
                for part in range(2):
                    most = far if part == way else far - 1
                    if dist > most:
                        continue
                    src = piece(h, part, dest, tall)
                    if dist < most:
                        held = ring.at[h, way, part, s - 2]
                        arrive(held, (sring, rring, (h, way, part, s - 2)))
                        held[...] += src[...]
                        src = held
                    at = (h, way, part, s - 1)
                    send(src, ring.at[at], (sring, rring, at), peer(sign))

    lax.fori_loop(0, HALF, count, 0)
    ring_step(1, (0,))
    pass_on(1)
    lax.fori_loop(0, ny, weigh_y, 0)
    lax.fori_loop(HALF, slots, count, 0)
    ring_step(1, (1,))
    pass_on(2)

    parts[...] = jnp.zeros_like(parts)
    edge = iota((SUB, rows), 0)
    xb[feats : feats + SUB, 0:rows] = jnp.where(edge == 0, 1.0, 0.0).astype(BF16)
    xb[feats : feats + SUB, rows : 2 * rows] = jnp.where(
        edge == 0, hess, jnp.where(edge == 1, grad, 0.0)
    ).astype(BF16)
    in_leaf = [jnp.where(leaf == lz * ny + f, 1.0, 0.0).astype(BF16) for lz in range(nz)]
    mine = leaf == iota((nz, rows), 0) * ny + f
    sum_h = jnp.sum(jnp.where(mine, hess, 0.0), axis=1, keepdims=True)
    sum_g = jnp.sum(jnp.where(mine, grad, 0.0), axis=1, keepdims=True)
    at_lane = iota((nz, LANES), 1)
    ends = jnp.where(at_lane == feats, sum_h, jnp.where(at_lane == feats + 1, sum_g, 0.0))

    for d in range(1, nx):
        at = lax.rem(x - d + nx, nx) * CORES + core
        arrive(xt.at[at], (sx, rx, (d - 1,)))
        send(xt.at[at], xt.at[at], (sx, rx, (nx - 1 + d,)), mate)
    steps = max(nz, ny) // 2
    ring_step(2, (0,))
    arrive(xt.at[f], (sx, rx, (nx - 1,)))
    for d in range(1, nx):
        at = lax.rem(x - d + nx, nx) * CORES + (1 - core)
        arrive(xt.at[at], (sx, rx, (nx - 1 + d,)))
    for b in range(nf):
        block = xt[b]
        cut = pl.ds(b * group, group)
        cut2 = pl.ds(rows + b * group, group)
        scaled = hess_ref[:, cut] * block
        xb[0:feats, cut] = block.astype(BF16)
        xb[0:feats, cut2] = scaled.astype(BF16)
    right = [jnp.concatenate([xb[0:feats, rows:] * m, xb[0:feats, :rows] * m], axis=1) for m in in_leaf]
    wide = dot(xb[...], jnp.concatenate(right, axis=0), NT)
    fold = feats // 2
    quarter = fold // 2
    span = (fold, nz * feats)
    behind = lax.rem(iota(span, 1), feats) - iota(span, 0)
    corner = pltpu.roll(wide[fold:feats], nz * feats - fold, 1)
    tri = jnp.where(behind < 0, corner, wide[0:fold])
    diag = jnp.sum(jnp.where(behind == 0, corner, 0.0), axis=0, keepdims=True)
    first = iota((1, LANES), 1) < feats
    lane = iota((1, LANES), 1)
    for t in range(nz // 2):
        cut = slice(t * LANES, (t + 1) * LANES)
        upper, lower = tri[0:quarter, cut], tri[quarter:fold, cut]
        edge = wide[feats : feats + 8, cut]
        turned = pltpu.roll(edge, feats, 1)
        even, odd = 2 * t, 2 * t + 1
        parts[even, 0:quarter, :] = jnp.where(first, upper, pltpu.roll(lower, feats, 1))
        parts[odd, 0:quarter, :] = jnp.where(first, pltpu.roll(upper, feats, 1), lower)
        parts[even, quarter : quarter + 1, :] = jnp.where(first, edge[0:1], turned[1:2])
        parts[odd, quarter : quarter + 1, :] = jnp.where(first, turned[0:1], edge[1:2])
        here = diag[:, cut]
        for lz, row in ((even, here), (odd, pltpu.roll(here, feats, 1))):
            parts[lz, quarter + 1 : quarter + 2, :] = jnp.where(first, row, ends[lz : lz + 1])
    heard(2)
    for k in range(1, nz):
        to = lax.rem(z + k, nz)
        send(parts.at[to], gram_z.at[k - 1], (sgz, rgz, (k - 1,)), at_z(k))

    ring_step(2, (1,))
    for s in range(3, steps):
        ring_step(s)

    total = parts[z]
    for k in range(1, nz):
        arrive(gram_z.at[k - 1], (sgz, rgz, (k - 1,)))
        total = total + gram_z[k - 1]
    gram_send[...] = total
    for k in range(1, ny):
        send(gram_send, gram_y.at[k - 1], (sgy, rgy, (k - 1,)), at_y(k))

    if steps > 2:
        ring_step(steps)

    for h, (n, me, peer, tall) in enumerate(axes):
        other, peer2 = (ny, at_y) if h == 0 else (nz, at_z)
        for part in range(2):
            out = piece(h, part, me, tall)[...]
            for way in range(2):
                far = n // 2 if part == way else n // 2 - 1
                if far > 0:
                    at = (h, way, part, n // 2 - 1)
                    arrive(ring.at[at], (sring, rring, at))
                    out = out + ring[at]
            for j in range(2):
                for gh in range(2):
                    slot = gh * HALF + part * 2 + j
                    for d in range(other):
                        spread[h, d, slot : slot + 1, :] = out[j, gh * other + d : gh * other + d + 1, :]
        here = y if h == 0 else z
        for k in range(1, other):
            to = lax.rem(here + k, other)
            send(spread.at[h, to], gathered.at[h, k - 1], (sh, rh, (h, k - 1)), peer2(k))

    for k in range(1, ny):
        arrive(gram_y.at[k - 1], (sgy, rgy, (k - 1,)))
        total = total + gram_y[k - 1]
    subs = iota((fold, LANES), 0)
    lanes = iota((fold, LANES), 1)
    turned = pltpu.roll(total[0:quarter], LANES - feats, 1)
    tri = jnp.concatenate([total[0:quarter], turned], axis=0)
    ends = total[quarter + 1 : quarter + 2]
    square[...] = jnp.zeros((LANES, LANES), F32)
    square[0:fold, :] = jnp.where(
        (lanes > subs) & (lanes < feats), tri, jnp.where(lanes == subs, 0.5 * tri, 0.0)
    )
    shifted = pltpu.roll(tri, fold, 1)
    far_diag = jnp.broadcast_to(pltpu.roll(ends, fold, 1), (fold, LANES))
    square[fold:feats, :] = jnp.where(
        (lanes >= fold) & (lanes < subs + fold), shifted,
        jnp.where(lanes == subs + fold, 0.5 * far_diag, 0.0),
    )
    edge = total[quarter : quarter + 1]
    square[feats : feats + 1, :] = jnp.where(lane < feats, edge, 0.0)
    square[feats + 1 : feats + 2, :] = jnp.where(
        lane < feats, pltpu.roll(edge, LANES - feats, 1), 0.0
    )
    square_t = square[...] + jnp.transpose(square[...])
    a = square_t[0:feats]
    lanes = iota((feats, LANES), 1)
    subs = iota((feats, LANES), 0)
    a = jnp.where(lanes <= feats, 0.5 * a, a) + jnp.where(lanes == subs, RIDGE_REG, 0.0)
    border = jnp.broadcast_to(a[:, feats : feats + 1], (feats, LANES))
    for k in range(0, feats, 2):
        c0 = jnp.broadcast_to(a[:, k : k + 1], (feats, LANES))
        c1 = jnp.broadcast_to(a[:, k + 1 : k + 2], (feats, LANES))
        r0, r1 = a[k : k + 1], a[k + 1 : k + 2]
        p00, p10 = c0[k : k + 1], c0[k + 1 : k + 2]
        p01, p11 = c1[k : k + 1], c1[k + 1 : k + 2]
        scale = 1.0 / (p00 * p11 - p01 * p10)
        n0 = (p11 * r0 - p01 * r1) * scale
        n1 = (p00 * r1 - p10 * r0) * scale
        a = a - c0 * n0 - c1 * n1
        a = jnp.where(subs == k, n0, jnp.where(subs == k + 1, n1, a))
    yc = jnp.broadcast_to(a[:, feats : feats + 1], (feats, LANES))
    yb = jnp.broadcast_to(a[:, feats + 1 : feats + 2], (feats, LANES))
    low = ends[:, feats : feats + 1] + RIDGE_REG - jnp.sum(border * yc, axis=0, keepdims=True)
    high = ends[:, feats + 1 : feats + 2] - jnp.sum(border * yb, axis=0, keepdims=True)
    const = high / low
    answer = jnp.sum(jnp.where(lanes == subs, yb - const * yc, 0.0), axis=0, keepdims=True)
    early = list(started)
    started.clear()
    own = f * nz + z
    coef_z[own] = -jnp.where(lane == feats, const, answer)

    def give(k, carry):
        dz = lax.rem(lax.div(k, nf) + nz // 2, nz)
        df = lax.rem(lax.rem(k, nf) + nf // 2, nf)

        @pl.when(dz + df > 0)
        def _():
            dev = (lax.rem(z + dz, nz) * ny + y, lax.rem(f + df, nf))
            pltpu.make_async_remote_copy(
                src_ref=coef_z.at[own], dst_ref=coef_z.at[own], send_sem=scz.at[0], recv_sem=rcz.at[0],
                device_id=dev, device_id_type=MESH,
            ).start()

        return carry

    lax.fori_loop(0, nz * nf, give, 0)
    shared = pltpu.make_async_remote_copy(
        src_ref=coef_z.at[pl.ds(0, nz * nf - 1)], dst_ref=coef_z.at[pl.ds(0, nz * nf - 1)],
        send_sem=scz.at[0], recv_sem=rcz.at[0], device_id=(row_pos, f), device_id_type=MESH,
    )

    upper = (iota((BINS, BINS), 0) <= iota((BINS, BINS), 1)).astype(F32).astype(BF16)
    gains = []
    for h in range(2):
        other = ny if h == 0 else nz
        sums = spread[h, y if h == 0 else z]
        for k in range(1, other):
            arrive(gathered.at[h, k - 1], (sh, rh, (h, k - 1)))
            sums = sums + gathered[h, k - 1]
        hi, mid, lo = split3(sums)
        run = dot(hi, upper, NN) + dot(mid, upper, NN) + dot(lo, upper, NN)
        lg, lh = run[0:HALF], run[HALF : 2 * HALF]
        tg, th = lg[:, BINS - 1 : BINS], lh[:, BINS - 1 : BINS]
        rg = tg - lg
        gains.append(
            lg * lg / (lh + SPLIT_REG) + rg * rg / (th - lh + SPLIT_REG) - tg * tg / (th + SPLIT_REG)
        )
    top = jnp.maximum(gains[0], gains[1])
    top = jnp.max(jnp.max(top, axis=1, keepdims=True), axis=0, keepdims=True)
    tops[f] = jnp.broadcast_to(top, (8, LANES))
    for k in range(1, nf):
        send(tops.at[f], tops.at[f], (stp, rtp, (k - 1,)), at_f(k))

    for copy in early:
        copy.wait_send()

    for k in range(1, nf):
        at = lax.rem(f - k + nf, nf)
        arrive(tops.at[at], (stp, rtp, (k - 1,)))
    best = tops[0]
    for k in range(1, nf):
        best = jnp.maximum(best, tops[k])
    best = best[0:1, 0:1]
    for h in range(2):
        gain_ref[0, h * HALF : (h + 1) * HALF, :] = gains[h] - best

    shared.wait_recv()
    coef_ref[...] = coef_z[y * nz + z][:, 0 : feats + 1]
    own_rows = leaf_ref[:, pl.ds(pl.multiple_of(f * group, group), group)]
    tables = jnp.concatenate([coef_z[k] for k in range(nz * nf)], axis=0)
    if leaves < LANES:
        tables = jnp.concatenate([tables, jnp.zeros((LANES - leaves, LANES), F32)], axis=0)
    column = jnp.transpose(tables)
    key = lax.rem(own_rows, ny) * nz + own_rows // ny
    pick = (iota((LANES, group), 0) == key).astype(F32).astype(BF16)
    hi, mid, lo = split3(column)
    per_row = dot(hi, pick, NN) + dot(mid, pick, NN) + dot(lo, pick, NN)
    value = jnp.sum(xt[f] * per_row[0:feats], axis=0, keepdims=True) + per_row[feats : feats + 1]
    score_ref[...] = prior_ref[...] + SHRINKAGE * value

    for copy in started:
        copy.wait_send()
    shared.wait_send()


def place(*refs):
    copies = [pltpu.make_async_copy(refs[i], refs[3 + i], refs[6].at[i]) for i in range(3)]
    for copy in copies:
        copy.start()
    for copy in copies:
        copy.wait()


def body(bin_ids, leaf_ids, gradient, hessian, raw_feats, prior_score, elected):
    rows = bin_ids.shape[1]
    leaves, slots = elected.shape
    nf = lax.axis_size("feat")
    ny = nf
    nz = lax.axis_size("rows") // ny
    group, feats = raw_feats.shape
    small = lambda width, kind: pltpu.VMEM((1, width), kind)
    nx = nf // CORES
    far = max(nz, ny)
    tall = 2 * ny
    dma = pltpu.SemaphoreType.DMA
    vmem = pltpu.VMEM
    scratch = [
        vmem((bin_ids.shape[0], rows), jnp.int32),
        small(rows, jnp.int32), small(rows, F32), small(rows, F32),
        vmem((feats, group), BF16), small(group, F32), vmem((slots, leaves), jnp.int32), dma((7,)),
        pltpu.SemaphoreType.REGULAR((max(nz, ny) // 2 - 1, 2)),
        vmem((nf, feats, group), F32),
        vmem((slots * SUB, rows), BF16),
        vmem((slots, rows), F32),
        vmem((2, 2 * leaves, rows), BF16),
        vmem((slots, 2 * leaves, BINS), F32),
        vmem((2, 2, 2, far // 2, 2, tall, BINS), F32),
        vmem((2, far, 2 * HALF, BINS), F32),
        vmem((2, far - 1, 2 * HALF, BINS), F32),
        vmem((feats + SUB, 2 * rows), BF16),
        vmem((nz, PACK, LANES), F32),
        vmem((nz - 1, PACK, LANES), F32),
        vmem((PACK, LANES), F32),
        vmem((ny - 1, PACK, LANES), F32),
        vmem((LANES, LANES), F32),
        vmem((nz * nf, 1, LANES), F32),
        vmem((nf, 8, LANES), F32),
    ]
    counts = [
        (2 * nx - 1,), (2, 2, 2, far // 2), (2, far - 1), (nz - 1,), (ny - 1,), (1,),
        (nf - 1,),
    ]
    for shape in counts:
        scratch += [dma(shape), dma(shape)]
    operands = (
        bin_ids, leaf_ids.reshape(1, rows), gradient.reshape(1, rows), hessian.reshape(1, rows),
        raw_feats.T, prior_score.reshape(1, group), elected.T,
    )
    operands = [pltpu.with_memory_space_constraint(v, pltpu.HBM) for v in operands]
    gain, coef, score = pl.pallas_call(
        functools.partial(kernel, (nz, ny, nf)),
        out_shape=(
            jax.ShapeDtypeStruct((1, slots, BINS), F32),
            jax.ShapeDtypeStruct((1, feats + 1), F32),
            jax.ShapeDtypeStruct((1, group), F32),
        ),
        in_specs=[pl.BlockSpec(memory_space=pltpu.HBM)] * 7,
        out_specs=(pl.BlockSpec(memory_space=pltpu.VMEM),) * 3,
        scratch_shapes=scratch,
        compiler_params=pltpu.CompilerParams(
            collective_id=0, has_side_effects=True, vmem_limit_bytes=50331648
        ),
        name="level",
    )(
        *operands
    )
    results = [pltpu.with_memory_space_constraint(v, pltpu.VMEM) for v in (gain, coef, score)]
    gain, coef, score = pl.pallas_call(
        place,
        out_shape=tuple(jax.ShapeDtypeStruct(r.shape, r.dtype) for r in results),
        in_specs=[pl.BlockSpec(memory_space=pltpu.VMEM)] * 3,
        out_specs=(pl.BlockSpec(memory_space=pltpu.HBM),) * 3,
        scratch_shapes=[dma((3,))],
        name="place",
    )(*results)
    return gain, coef, score.reshape(group)


def solution(mesh):
    in_specs = (
        P("feat", "rows"),
        P("rows"),
        P("rows"),
        P("rows"),
        P(("rows", "feat"), None),
        P(("rows", "feat")),
        P(None, "feat"),
    )
    out_specs = (P("rows", "feat", None), P("rows", None), P(("rows", "feat")))
    return jax.shard_map(body, mesh=mesh, in_specs=in_specs, out_specs=out_specs, check_vma=False)
```
